256 devices in a mesh: row: 32 (over x_lo, z, core), col: 8 (over y, x_hi).
Axes of the slice: x: 4 (x_hi: 2, x_lo: 2; x = x_hi * 2 + x_lo), y: 4, z: 8, core: 2. Of those that a mesh axis runs over, the one named last changes fastest.
Arguments:
- maps: bfloat16 [48, 1024, 1024], P(None, 'row', 'col'), may hold values from -6 to 6
- kernel: bfloat16 [3, 3, 48, 48], replicated, may hold values from -0.3125 to 0.3125
- mixing: bfloat16 [48, 48], replicated, may hold values from -0.875 to 0.875
- cotangent: bfloat16 [48, 1024, 1024], P(None, 'row', 'col'), may hold values from -6 to 6
Outputs:
- output: bfloat16 [48, 1024, 1024], P(None, 'row', 'col')
- grad_maps: bfloat16 [48, 1024, 1024], P(None, 'row', 'col')
- grad_kernel: float32 [3, 3, 48, 48], replicated
- grad_mixing: float32 [48, 48], replicated
The draws below stay inside these ranges and needn't reach their ends.
All inputs are finite; a program needn't handle non-finite values.
Results may differ from the reference program's by a relative error of at most 0.0056.
Values may be sent and summed in bfloat16 or wider, within the bound.
A program may use at most 128 MiB of HBM per device.

```python
import jax
import jax.numpy as jnp
from jax import lax

CHANNELS = 48
DILATION = 8
MAP_BINS = 1024


def level_of(own_key, extent, cuts, smallest, high):
    factor_of = 1.0
    for position, shards_of in cuts:
        heights = jax.random.uniform(jax.random.fold_in(jax.random.fold_in(own_key, 6), position), (shards_of,), jnp.float32, smallest / len(cuts), high / len(cuts))
        factor_of = factor_of * jnp.repeat(jnp.exp(heights), extent[position] // shards_of).reshape((-1,) + (1,) * (len(extent) - 1 - position))
    return factor_of


def gaussian(key, shape, spread, most, shards=(), held_as=jnp.bfloat16):
    factor_of = level_of(key, shape, shards, -0.22, 0.18) if shards else 1.0
    array = jax.random.normal(key, shape, jnp.float32) * spread * factor_of
    return jnp.minimum(jnp.maximum(array, -most), most).astype(held_as)


def setup_inputs(seed: int = 0) -> dict:
    key_list = jax.random.split(jax.random.key(seed), 5)
    return {
        "maps": gaussian(key_list[0], (CHANNELS, MAP_BINS, MAP_BINS), 1.0, 6.0, ((1, 32), (2, 8))),
        "kernel": gaussian(key_list[1], (3, 3, CHANNELS, CHANNELS), (9 * CHANNELS) ** -0.5, 0.3125),
        "mixing": gaussian(key_list[2], (CHANNELS, CHANNELS), CHANNELS ** -0.5, 0.875),
        "cotangent": gaussian(key_list[3], (CHANNELS, MAP_BINS, MAP_BINS), 1.0, 6.0, ((1, 32), (2, 8))),
    }


def convolve(active, kernel):
    return lax.conv_general_dilated(active[None], jnp.transpose(kernel, (3, 2, 0, 1)), (1, 1), ((DILATION, DILATION), (DILATION, DILATION)), rhs_dilation=(DILATION, DILATION), dimension_numbers=('NCHW', 'OIHW', 'NCHW'), precision=lax.Precision.HIGHEST)[0]

def reference(maps, kernel, mixing, cotangent):
    highest = lax.Precision.HIGHEST
    active = jnp.maximum(maps, 0).astype(jnp.float32)
    kernel_wide = kernel.astype(jnp.float32)
    before, pullback = jax.vjp(convolve, active, kernel_wide)
    hidden = jnp.maximum(before, 0.0).astype(jnp.bfloat16)
    hidden_wide = lax.optimization_barrier(hidden).astype(jnp.float32)
    mixing_wide = mixing.astype(jnp.float32)
    mixed = jnp.einsum('io,ihw->ohw', mixing_wide, hidden_wide, precision=highest).astype(jnp.bfloat16)
    mixed_wide = lax.optimization_barrier(mixed).astype(jnp.float32)
    output = (maps.astype(jnp.float32) + 0.5 * (mixed_wide + jnp.swapaxes(mixed_wide, 1, 2))).astype(jnp.bfloat16)
    grad_wide = cotangent.astype(jnp.float32)
    grad_mixed = (0.5 * (grad_wide + jnp.swapaxes(grad_wide, 1, 2))).astype(jnp.bfloat16)
    grad_mixed = lax.optimization_barrier(grad_mixed).astype(jnp.float32)
    grad_mixing = jnp.einsum('ihw,ohw->io', hidden_wide, grad_mixed, precision=highest)
    grad_hidden = jnp.einsum('io,ohw->ihw', mixing_wide, grad_mixed, precision=highest)
    grad_before = jnp.where(hidden > 0, grad_hidden, 0.0).astype(jnp.bfloat16)
    grad_before = lax.optimization_barrier(grad_before).astype(jnp.float32)
    grad_active, grad_kernel = pullback(grad_before)
    grad_maps = (grad_wide + jnp.where(maps > 0, grad_active, 0.0)).astype(jnp.bfloat16)
    return (output, grad_maps, grad_kernel / MAP_BINS, grad_mixing / MAP_BINS)
```

```python
import jax
import jax.numpy as jnp
from jax import lax
from jax.sharding import PartitionSpec as P

DILATION = 8


def with_halo(array, sides, width):
    for axis, dim in sides:
        peers, length = (lax.axis_size(axis), array.shape[dim])
        up = [(i, (i + 1) % peers) for i in range(peers - 1)]
        down = [(j, i) for i, j in up]
        last = lax.slice_in_dim(array, length - width, length, axis=dim)
        initial = lax.slice_in_dim(array, 0, width, axis=dim)
        before = lax.ppermute(last, axis, up)
        after = lax.ppermute(initial, axis, down)
        array = jnp.concatenate([before, array, after], axis=dim)
    return array


def all_sum(x, axes):
    for axis in axes:
        peers = lax.axis_size(axis)
        if peers & (peers - 1):
            x = lax.psum(x, axis)
            continue
        step = 1
        while step < peers:
            x = x + lax.ppermute(x, axis, [(i, i ^ step) for i in range(peers)])
            step *= 2
    return x


def mirror_tile(tile):
    row_count = lax.axis_size("row")
    col_count = lax.axis_size("col")
    chans, rows, cols = tile.shape
    width = rows // col_count
    strip = lax.all_to_all(tile, "col", split_axis=1, concat_axis=2, tiled=True)
    blocks = lax.all_to_all(strip, "row", split_axis=2, concat_axis=1, tiled=True)
    turned = jnp.transpose(blocks.reshape(chans, row_count, width, rows), (0, 3, 1, 2))
    landed = lax.all_to_all(turned, "col", split_axis=2, concat_axis=3, tiled=True)
    return landed.reshape(chans, rows, cols)


def window(padded, top, left, rows, cols):
    return padded[:, top : top + rows, left : left + cols]


def shards(maps, kernel, mixing, cotangent):
    chans, rows, cols = maps.shape
    map_bins = rows * lax.axis_size("row")
    active = jnp.maximum(maps, 0)
    padded = with_halo(active, (("row", 1), ("col", 2)), DILATION)
    before = jnp.zeros((chans, rows, cols), jnp.float32)
    for row_tap in range(3):
        for col_tap in range(3):
            piece = window(padded, DILATION * row_tap, DILATION * col_tap, rows, cols)
            before = before + jnp.einsum(
                "io,ihw->ohw", kernel[row_tap, col_tap], piece, preferred_element_type=jnp.float32
            )
    hidden = jnp.maximum(before, 0.0).astype(jnp.bfloat16)
    mixed = jnp.einsum("io,ihw->ohw", mixing, hidden, preferred_element_type=jnp.float32).astype(
        jnp.bfloat16
    )
    mixed_turned = mirror_tile(mixed)
    grad_turned = mirror_tile(cotangent)
    output = (
        maps.astype(jnp.float32)
        + 0.5 * (mixed.astype(jnp.float32) + mixed_turned.astype(jnp.float32))
    ).astype(jnp.bfloat16)
    grad_wide = cotangent.astype(jnp.float32)
    grad_mixed = (0.5 * (grad_wide + grad_turned.astype(jnp.float32))).astype(jnp.bfloat16)
    local_mixing = jnp.einsum("ihw,ohw->io", hidden, grad_mixed, preferred_element_type=jnp.float32)
    grad_hidden = jnp.einsum("io,ohw->ihw", mixing, grad_mixed, preferred_element_type=jnp.float32)
    grad_before = jnp.where(hidden > 0, grad_hidden, 0.0).astype(jnp.bfloat16)
    tap_grads = []
    for row_tap in range(3):
        for col_tap in range(3):
            piece = window(padded, DILATION * row_tap, DILATION * col_tap, rows, cols)
            tap_grads.append(
                jnp.einsum("ihw,ohw->io", piece, grad_before, preferred_element_type=jnp.float32)
            )
    local_kernel = jnp.stack(tap_grads).reshape(3, 3, chans, chans)
    sums = all_sum(jnp.concatenate([local_kernel.reshape(9, chans, chans), local_mixing[None]]), ("row", "col"))
    grad_kernel, grad_mixing = sums[:9].reshape(3, 3, chans, chans), sums[9]
    grad_padded = with_halo(grad_before, (("row", 1), ("col", 2)), DILATION)
    grad_active = jnp.zeros((chans, rows, cols), jnp.float32)
    for row_tap in range(3):
        for col_tap in range(3):
            piece = window(
                grad_padded,
                2 * DILATION - DILATION * row_tap,
                2 * DILATION - DILATION * col_tap,
                rows,
                cols,
            )
            grad_active = grad_active + jnp.einsum(
                "io,ohw->ihw", kernel[row_tap, col_tap], piece, preferred_element_type=jnp.float32
            )
    grad_maps = (grad_wide + jnp.where(maps > 0, grad_active, 0.0)).astype(jnp.bfloat16)
    return (output, grad_maps, grad_kernel / map_bins, grad_mixing / map_bins)


def solution(mesh):
    placed = (P(None, "row", "col"), P(), P(), P(None, "row", "col"))
    return jax.shard_map(
        shards,
        mesh=mesh,
        in_specs=placed,
        out_specs=(P(None, "row", "col"), P(None, "row", "col"), P(), P()),
        check_vma=False,
    )
```

```python
import jax
import jax.numpy as jnp
from jax import lax
from jax.sharding import PartitionSpec as P

DILATION = 8


def with_halo(array, sides, width):
    for axis, dim in sides:
        peers, length = (lax.axis_size(axis), array.shape[dim])
        up = [(i, (i + 1) % peers) for i in range(peers - 1)]
        down = [(j, i) for i, j in up]
        last = lax.slice_in_dim(array, length - width, length, axis=dim)
        initial = lax.slice_in_dim(array, 0, width, axis=dim)
        before = lax.ppermute(last, axis, up)
        after = lax.ppermute(initial, axis, down)
        array = jnp.concatenate([before, array, after], axis=dim)
    return array


def all_sum(x, axes):
    for axis in axes:
        peers = lax.axis_size(axis)
        if peers & (peers - 1):
            x = lax.psum(x, axis)
            continue
        step = 1
        while step < peers:
            x = x + lax.ppermute(x, axis, [(i, i ^ step) for i in range(peers)])
            step *= 2
    return x


def mirror_tile(tile):
    row_count = lax.axis_size("row")
    col_count = lax.axis_size("col")
    chans, rows, cols = tile.shape
    width = rows // col_count
    strip = lax.all_to_all(tile, "col", split_axis=1, concat_axis=2, tiled=True)
    blocks = lax.all_to_all(strip, "row", split_axis=2, concat_axis=1, tiled=True)
    turned = jnp.transpose(blocks.reshape(chans, row_count, width, rows), (0, 3, 1, 2))
    landed = lax.all_to_all(turned, "col", split_axis=2, concat_axis=3, tiled=True)
    return landed.reshape(chans, rows, cols)


def window(padded, top, left, rows, cols):
    return padded[:, top : top + rows, left : left + cols]


def shards(maps, kernel, mixing, cotangent):
    chans, rows, cols = maps.shape
    map_bins = rows * lax.axis_size("row")
    active = jnp.maximum(maps, 0)
    padded = with_halo(active, (("row", 1), ("col", 2)), DILATION)
    before = jnp.zeros((chans, rows, cols), jnp.float32)
    for row_tap in range(3):
        for col_tap in range(3):
            piece = window(padded, DILATION * row_tap, DILATION * col_tap, rows, cols)
            before = before + jnp.einsum(
                "io,ihw->ohw", kernel[row_tap, col_tap], piece, preferred_element_type=jnp.float32
            )
    hidden = jnp.maximum(before, 0.0).astype(jnp.bfloat16)
    mixed = jnp.einsum("io,ihw->ohw", mixing, hidden, preferred_element_type=jnp.float32).astype(
        jnp.bfloat16
    )
    mixed_turned = mirror_tile(mixed)
    grad_turned = mirror_tile(cotangent)
    output = (
        maps.astype(jnp.float32)
        + 0.5 * (mixed.astype(jnp.float32) + mixed_turned.astype(jnp.float32))
    ).astype(jnp.bfloat16)
    grad_wide = cotangent.astype(jnp.float32)
    grad_mixed = (0.5 * (grad_wide + grad_turned.astype(jnp.float32))).astype(jnp.bfloat16)
    local_mixing = jnp.einsum("ihw,ohw->io", hidden, grad_mixed, preferred_element_type=jnp.float32)
    grad_hidden = jnp.einsum("io,ohw->ihw", mixing, grad_mixed, preferred_element_type=jnp.float32)
    grad_before = jnp.where(hidden > 0, grad_hidden, 0.0).astype(jnp.bfloat16)
    tap_grads = []
    for row_tap in range(3):
        for col_tap in range(3):
            piece = window(padded, DILATION * row_tap, DILATION * col_tap, rows, cols)
            tap_grads.append(
                jnp.einsum("ihw,ohw->io", piece, grad_before, preferred_element_type=jnp.float32)
            )
    local_kernel = jnp.stack(tap_grads).reshape(3, 3, chans, chans)
    flat = jnp.concatenate([local_kernel.reshape(-1), local_mixing.reshape(-1)])
    sums = all_sum(flat.reshape(-1, 128), ("row", "col")).reshape(-1)
    grad_kernel = sums[: 9 * chans * chans].reshape(3, 3, chans, chans)
    grad_mixing = sums[9 * chans * chans :].reshape(chans, chans)
    grad_padded = with_halo(grad_before, (("row", 1), ("col", 2)), DILATION)
    grad_active = jnp.zeros((chans, rows, cols), jnp.float32)
    for row_tap in range(3):
        for col_tap in range(3):
            piece = window(
                grad_padded,
                2 * DILATION - DILATION * row_tap,
                2 * DILATION - DILATION * col_tap,
                rows,
                cols,
            )
            grad_active = grad_active + jnp.einsum(
                "io,ohw->ihw", kernel[row_tap, col_tap], piece, preferred_element_type=jnp.float32
            )
    grad_maps = (grad_wide + jnp.where(maps > 0, grad_active, 0.0)).astype(jnp.bfloat16)
    return (output, grad_maps, grad_kernel / map_bins, grad_mixing / map_bins)


def solution(mesh):
    placed = (P(None, "row", "col"), P(), P(), P(None, "row", "col"))
    return jax.shard_map(
        shards,
        mesh=mesh,
        in_specs=placed,
        out_specs=(P(None, "row", "col"), P(None, "row", "col"), P(), P()),
        check_vma=False,
    )
```

```python
import jax
import jax.numpy as jnp
from jax import lax
from jax.sharding import PartitionSpec as P

DILATION = 8


def with_halo(array, sides, width):
    for axis, dim in sides:
        peers, length = (lax.axis_size(axis), array.shape[dim])
        up = [(i, (i + 1) % peers) for i in range(peers - 1)]
        down = [(j, i) for i, j in up]
        last = lax.slice_in_dim(array, length - width, length, axis=dim)
        initial = lax.slice_in_dim(array, 0, width, axis=dim)
        before = lax.ppermute(last, axis, up)
        after = lax.ppermute(initial, axis, down)
        array = jnp.concatenate([before, array, after], axis=dim)
    return array


def all_sum(x, axes):
    for axis in axes:
        peers = lax.axis_size(axis)
        if peers & (peers - 1):
            x = lax.psum(x, axis)
            continue
        step = 1
        while step < peers:
            x = x + lax.ppermute(x, axis, [(i, i ^ step) for i in range(peers)])
            step *= 2
    return x


def mirror_tile(tile):
    row_count = lax.axis_size("row")
    col_count = lax.axis_size("col")
    chans, rows, cols = tile.shape
    group = cols // rows
    turn = lax.axis_index("row") % group
    pieces = jnp.roll(tile.reshape(chans, rows, group, rows), -turn, axis=2)
    landed = []
    for k in range(group):
        piece = jnp.swapaxes(pieces[:, :, k, :], 1, 2).reshape(chans, rows * rows)
        pairs = []
        for source_row in range(row_count):
            for source_col in range(col_count):
                target_row = group * source_col + (source_row % group + k) % group
                target = target_row * col_count + source_row // group
                pairs.append((source_row * col_count + source_col, target))
        landed.append(lax.ppermute(piece, ("row", "col"), pairs).reshape(chans, rows, rows))
    slots = jnp.stack([landed[(-i) % group] for i in range(group)], axis=2)
    return jnp.roll(slots, turn, axis=2).reshape(chans, rows, cols)


def window(padded, top, left, rows, cols):
    return padded[:, top : top + rows, left : left + cols]


def shards(maps, kernel, mixing, cotangent):
    chans, rows, cols = maps.shape
    map_bins = rows * lax.axis_size("row")
    active = jnp.maximum(maps, 0)
    padded = with_halo(active, (("row", 1), ("col", 2)), DILATION)
    before = jnp.zeros((chans, rows, cols), jnp.float32)
    for row_tap in range(3):
        for col_tap in range(3):
            piece = window(padded, DILATION * row_tap, DILATION * col_tap, rows, cols)
            before = before + jnp.einsum(
                "io,ihw->ohw", kernel[row_tap, col_tap], piece, preferred_element_type=jnp.float32
            )
    hidden = jnp.maximum(before, 0.0).astype(jnp.bfloat16)
    mixed = jnp.einsum("io,ihw->ohw", mixing, hidden, preferred_element_type=jnp.float32).astype(
        jnp.bfloat16
    )
    mixed_turned = mirror_tile(mixed)
    grad_turned = mirror_tile(cotangent)
    output = (
        maps.astype(jnp.float32)
        + 0.5 * (mixed.astype(jnp.float32) + mixed_turned.astype(jnp.float32))
    ).astype(jnp.bfloat16)
    grad_wide = cotangent.astype(jnp.float32)
    grad_mixed = (0.5 * (grad_wide + grad_turned.astype(jnp.float32))).astype(jnp.bfloat16)
    local_mixing = jnp.einsum("ihw,ohw->io", hidden, grad_mixed, preferred_element_type=jnp.float32)
    grad_hidden = jnp.einsum("io,ohw->ihw", mixing, grad_mixed, preferred_element_type=jnp.float32)
    grad_before = jnp.where(hidden > 0, grad_hidden, 0.0).astype(jnp.bfloat16)
    tap_grads = []
    for row_tap in range(3):
        for col_tap in range(3):
            piece = window(padded, DILATION * row_tap, DILATION * col_tap, rows, cols)
            tap_grads.append(
                jnp.einsum("ihw,ohw->io", piece, grad_before, preferred_element_type=jnp.float32)
            )
    local_kernel = jnp.stack(tap_grads).reshape(3, 3, chans, chans)
    flat = jnp.concatenate([local_kernel.reshape(-1), local_mixing.reshape(-1)])
    sums = all_sum(flat.reshape(-1, 128), ("row", "col")).reshape(-1)
    grad_kernel = sums[: 9 * chans * chans].reshape(3, 3, chans, chans)
    grad_mixing = sums[9 * chans * chans :].reshape(chans, chans)
    grad_padded = with_halo(grad_before, (("row", 1), ("col", 2)), DILATION)
    grad_active = jnp.zeros((chans, rows, cols), jnp.float32)
    for row_tap in range(3):
        for col_tap in range(3):
            piece = window(
                grad_padded,
                2 * DILATION - DILATION * row_tap,
                2 * DILATION - DILATION * col_tap,
                rows,
                cols,
            )
            grad_active = grad_active + jnp.einsum(
                "io,ohw->ihw", kernel[row_tap, col_tap], piece, preferred_element_type=jnp.float32
            )
    grad_maps = (grad_wide + jnp.where(maps > 0, grad_active, 0.0)).astype(jnp.bfloat16)
    return (output, grad_maps, grad_kernel / map_bins, grad_mixing / map_bins)


def solution(mesh):
    placed = (P(None, "row", "col"), P(), P(), P(None, "row", "col"))
    return jax.shard_map(
        shards,
        mesh=mesh,
        in_specs=placed,
        out_specs=(P(None, "row", "col"), P(None, "row", "col"), P(), P()),
        check_vma=False,
    )
```

```python
import functools

import jax
import jax.numpy as jnp
from jax import lax
from jax.experimental import pallas as pl
from jax.experimental.pallas import tpu as pltpu
from jax.sharding import PartitionSpec as P

DILATION = 8


def with_halo(array, sides, width):
    for axis, dim in sides:
        peers, length = (lax.axis_size(axis), array.shape[dim])
        up = [(i, (i + 1) % peers) for i in range(peers - 1)]
        down = [(j, i) for i, j in up]
        last = lax.slice_in_dim(array, length - width, length, axis=dim)
        initial = lax.slice_in_dim(array, 0, width, axis=dim)
        before = lax.ppermute(last, axis, up)
        after = lax.ppermute(initial, axis, down)
        array = jnp.concatenate([before, array, after], axis=dim)
    return array


def flip(index, stride):
    return index + stride - 2 * stride * ((index // stride) % 2)


def sum_kernel(strides, x_ref, out_ref, arrived, partial, send_sem, recv_sem):
    row, col = lax.axis_index("row"), lax.axis_index("col")
    partners = [(flip(row, stride), col) if axis == "row" else (row, flip(col, stride)) for axis, stride in strides]
    barrier = pltpu.get_barrier_semaphore()
    for partner in partners:
        pl.semaphore_signal(barrier, inc=1, device_id=partner, device_id_type=pl.DeviceIdType.MESH)
    pl.semaphore_wait(barrier, len(partners))
    source = x_ref
    for step, partner in enumerate(partners):
        copy = pltpu.make_async_remote_copy(
            src_ref=source,
            dst_ref=arrived.at[step],
            send_sem=send_sem.at[step],
            recv_sem=recv_sem.at[step],
            device_id=partner,
            device_id_type=pl.DeviceIdType.MESH,
        )
        copy.start()
        copy.wait()
        target = out_ref if step == len(partners) - 1 else partial.at[step]
        target[...] = source[...] + arrived[step]
        source = target


def all_sum(x):
    strides = []
    for axis in ("row", "col"):
        peers = lax.axis_size(axis)
        stride = 1
        while stride < peers:
            strides.append((axis, stride))
            stride *= 2
    count = len(strides)
    return pl.pallas_call(
        functools.partial(sum_kernel, strides),
        out_shape=jax.ShapeDtypeStruct(x.shape, x.dtype),
        in_specs=[pl.BlockSpec(memory_space=pltpu.VMEM)],
        out_specs=pl.BlockSpec(memory_space=pltpu.VMEM),
        scratch_shapes=[
            pltpu.VMEM((count,) + x.shape, x.dtype),
            pltpu.VMEM((count,) + x.shape, x.dtype),
            pltpu.SemaphoreType.DMA((count,)),
            pltpu.SemaphoreType.DMA((count,)),
        ],
        compiler_params=pltpu.CompilerParams(collective_id=0, has_side_effects=True),
    )(x)


def mirror_tile(tile):
    row_count = lax.axis_size("row")
    col_count = lax.axis_size("col")
    chans, rows, cols = tile.shape
    group = cols // rows
    turn = lax.axis_index("row") % group
    pieces = jnp.roll(tile.reshape(chans, rows, group, rows), -turn, axis=2)
    landed = []
    for k in range(group):
        piece = jnp.swapaxes(pieces[:, :, k, :], 1, 2).reshape(chans, rows * rows)
        pairs = []
        for source_row in range(row_count):
            for source_col in range(col_count):
                target_row = group * source_col + (source_row % group + k) % group
                target = target_row * col_count + source_row // group
                pairs.append((source_row * col_count + source_col, target))
        landed.append(lax.ppermute(piece, ("row", "col"), pairs).reshape(chans, rows, rows))
    slots = jnp.stack([landed[(-i) % group] for i in range(group)], axis=2)
    return jnp.roll(slots, turn, axis=2).reshape(chans, rows, cols)


def window(padded, top, left, rows, cols):
    return padded[:, top : top + rows, left : left + cols]


def shards(maps, kernel, mixing, cotangent):
    chans, rows, cols = maps.shape
    map_bins = rows * lax.axis_size("row")
    active = jnp.maximum(maps, 0)
    padded = with_halo(active, (("row", 1), ("col", 2)), DILATION)
    before = jnp.zeros((chans, rows, cols), jnp.float32)
    for row_tap in range(3):
        for col_tap in range(3):
            piece = window(padded, DILATION * row_tap, DILATION * col_tap, rows, cols)
            before = before + jnp.einsum(
                "io,ihw->ohw", kernel[row_tap, col_tap], piece, preferred_element_type=jnp.float32
            )
    hidden = jnp.maximum(before, 0.0).astype(jnp.bfloat16)
    mixed = jnp.einsum("io,ihw->ohw", mixing, hidden, preferred_element_type=jnp.float32).astype(
        jnp.bfloat16
    )
    mixed_turned = mirror_tile(mixed)
    grad_turned = mirror_tile(cotangent)
    output = (
        maps.astype(jnp.float32)
        + 0.5 * (mixed.astype(jnp.float32) + mixed_turned.astype(jnp.float32))
    ).astype(jnp.bfloat16)
    grad_wide = cotangent.astype(jnp.float32)
    grad_mixed = (0.5 * (grad_wide + grad_turned.astype(jnp.float32))).astype(jnp.bfloat16)
    local_mixing = jnp.einsum("ihw,ohw->io", hidden, grad_mixed, preferred_element_type=jnp.float32)
    grad_hidden = jnp.einsum("io,ohw->ihw", mixing, grad_mixed, preferred_element_type=jnp.float32)
    grad_before = jnp.where(hidden > 0, grad_hidden, 0.0).astype(jnp.bfloat16)
    tap_grads = []
    for row_tap in range(3):
        for col_tap in range(3):
            piece = window(padded, DILATION * row_tap, DILATION * col_tap, rows, cols)
            tap_grads.append(
                jnp.einsum("ihw,ohw->io", piece, grad_before, preferred_element_type=jnp.float32)
            )
    local_kernel = jnp.stack(tap_grads).reshape(3, 3, chans, chans)
    flat = jnp.concatenate([local_kernel.reshape(-1), local_mixing.reshape(-1)])
    sums = all_sum(flat.reshape(-1, 128)).reshape(-1)
    grad_kernel = sums[: 9 * chans * chans].reshape(3, 3, chans, chans)
    grad_mixing = sums[9 * chans * chans :].reshape(chans, chans)
    grad_padded = with_halo(grad_before, (("row", 1), ("col", 2)), DILATION)
    grad_active = jnp.zeros((chans, rows, cols), jnp.float32)
    for row_tap in range(3):
        for col_tap in range(3):
            piece = window(
                grad_padded,
                2 * DILATION - DILATION * row_tap,
                2 * DILATION - DILATION * col_tap,
                rows,
                cols,
            )
            grad_active = grad_active + jnp.einsum(
                "io,ohw->ihw", kernel[row_tap, col_tap], piece, preferred_element_type=jnp.float32
            )
    grad_maps = (grad_wide + jnp.where(maps > 0, grad_active, 0.0)).astype(jnp.bfloat16)
    return (output, grad_maps, grad_kernel / map_bins, grad_mixing / map_bins)


def solution(mesh):
    placed = (P(None, "row", "col"), P(), P(), P(None, "row", "col"))
    return jax.shard_map(
        shards,
        mesh=mesh,
        in_specs=placed,
        out_specs=(P(None, "row", "col"), P(None, "row", "col"), P(), P()),
        check_vma=False,
    )
```

```python
import functools

import jax
import jax.numpy as jnp
from jax import lax
from jax.experimental import pallas as pl
from jax.experimental.pallas import tpu as pltpu
from jax.sharding import PartitionSpec as P

DILATION = 8


def with_halo(array, sides, width):
    for axis, dim in sides:
        peers, length = (lax.axis_size(axis), array.shape[dim])
        up = [(i, (i + 1) % peers) for i in range(peers - 1)]
        down = [(j, i) for i, j in up]
        last = lax.slice_in_dim(array, length - width, length, axis=dim)
        initial = lax.slice_in_dim(array, 0, width, axis=dim)
        before = lax.ppermute(last, axis, up)
        after = lax.ppermute(initial, axis, down)
        array = jnp.concatenate([before, array, after], axis=dim)
    return array


def flip(index, stride):
    return index + stride - 2 * stride * ((index // stride) % 2)


def sum_kernel(strides, x_ref, out_ref, arrived, partial, send_sem, recv_sem):
    row, col = lax.axis_index("row"), lax.axis_index("col")
    partners = [(flip(row, stride), col) if axis == "row" else (row, flip(col, stride)) for axis, stride in strides]
    barrier = pltpu.get_barrier_semaphore()
    for partner in partners:
        pl.semaphore_signal(barrier, inc=1, device_id=partner, device_id_type=pl.DeviceIdType.MESH)
    pl.semaphore_wait(barrier, len(partners))
    source = x_ref
    for step, partner in enumerate(partners):
        copy = pltpu.make_async_remote_copy(
            src_ref=source,
            dst_ref=arrived.at[step],
            send_sem=send_sem.at[step],
            recv_sem=recv_sem.at[step],
            device_id=partner,
            device_id_type=pl.DeviceIdType.MESH,
        )
        copy.start()
        copy.wait()
        target = out_ref if step == len(partners) - 1 else partial.at[step]
        target[...] = source[...] + arrived[step]
        source = target


def all_sum(x):
    strides = []
    for axis in ("row", "col"):
        peers = lax.axis_size(axis)
        stride = 1
        while stride < peers:
            strides.append((axis, stride))
            stride *= 2
    count = len(strides)
    return pl.pallas_call(
        functools.partial(sum_kernel, strides),
        out_shape=jax.ShapeDtypeStruct(x.shape, x.dtype),
        in_specs=[pl.BlockSpec(memory_space=pltpu.VMEM)],
        out_specs=pl.BlockSpec(memory_space=pltpu.VMEM),
        scratch_shapes=[
            pltpu.VMEM((count,) + x.shape, x.dtype),
            pltpu.VMEM((count,) + x.shape, x.dtype),
            pltpu.SemaphoreType.DMA((count,)),
            pltpu.SemaphoreType.DMA((count,)),
        ],
        compiler_params=pltpu.CompilerParams(collective_id=0, has_side_effects=True),
    )(x)


def mirror_kernel(group, slabs_ref, out_ref, send_sem, recv_sem, local_sem):
    row, col = lax.axis_index("row"), lax.axis_index("col")
    turn = row % group
    own = row // group == col
    targets = [(group * col + (turn + k) % group, row // group) for k in range(group)]
    sources = [(group * col + (turn - k + group) % group, row // group) for k in range(group)]
    barrier = pltpu.get_barrier_semaphore()
    for k in range(group):
        if k == 0:
            @pl.when(jnp.logical_not(own))
            def _():
                pl.semaphore_signal(barrier, inc=1, device_id=sources[0], device_id_type=pl.DeviceIdType.MESH)
        else:
            pl.semaphore_signal(barrier, inc=1, device_id=sources[k], device_id_type=pl.DeviceIdType.MESH)
    pl.semaphore_wait(barrier, group - own.astype(jnp.int32))
    copies = []
    for k in range(group):
        copy = pltpu.make_async_remote_copy(
            src_ref=slabs_ref.at[k],
            dst_ref=out_ref.at[turn],
            send_sem=send_sem.at[k],
            recv_sem=recv_sem.at[k],
            device_id=targets[k],
            device_id_type=pl.DeviceIdType.MESH,
        )
        landing = pltpu.make_async_remote_copy(
            src_ref=slabs_ref.at[k],
            dst_ref=out_ref.at[(turn - k + group) % group],
            send_sem=send_sem.at[k],
            recv_sem=recv_sem.at[k],
            device_id=sources[k],
            device_id_type=pl.DeviceIdType.MESH,
        )
        copies.append((copy, landing))
    local = pltpu.make_async_copy(slabs_ref.at[0], out_ref.at[turn], local_sem)

    @pl.when(own)
    def _():
        local.start()

    @pl.when(jnp.logical_not(own))
    def _():
        copies[0][0].start()

    for copy, _ in copies[1:]:
        copy.start()

    @pl.when(own)
    def _():
        local.wait()

    @pl.when(jnp.logical_not(own))
    def _():
        copies[0][0].wait_send()
        copies[0][1].wait_recv()

    for copy, landing in copies[1:]:
        copy.wait_send()
        landing.wait_recv()


def mirror_tile(tile):
    chans, rows, cols = tile.shape
    group = cols // rows
    turn = lax.axis_index("row") % group
    pieces = jnp.roll(tile.reshape(chans, rows, group, rows), -turn, axis=2)
    slabs = jnp.stack([jnp.swapaxes(pieces[:, :, k, :], 1, 2).reshape(chans, rows * rows) for k in range(group)])
    landed = pl.pallas_call(
        functools.partial(mirror_kernel, group),
        out_shape=jax.ShapeDtypeStruct(slabs.shape, slabs.dtype),
        in_specs=[pl.BlockSpec(memory_space=pltpu.VMEM)],
        out_specs=pl.BlockSpec(memory_space=pltpu.VMEM),
        scratch_shapes=[
            pltpu.SemaphoreType.DMA((group,)),
            pltpu.SemaphoreType.DMA((group,)),
            pltpu.SemaphoreType.DMA,
        ],
        compiler_params=pltpu.CompilerParams(collective_id=1, has_side_effects=True),
    )(slabs)
    landed = landed.reshape(group, chans, rows, rows)
    return jnp.transpose(landed, (1, 2, 0, 3)).reshape(chans, rows, cols)


def window(padded, top, left, rows, cols):
    return padded[:, top : top + rows, left : left + cols]


def shards(maps, kernel, mixing, cotangent):
    chans, rows, cols = maps.shape
    map_bins = rows * lax.axis_size("row")
    active = jnp.maximum(maps, 0)
    padded = with_halo(active, (("row", 1), ("col", 2)), DILATION)
    before = jnp.zeros((chans, rows, cols), jnp.float32)
    for row_tap in range(3):
        for col_tap in range(3):
            piece = window(padded, DILATION * row_tap, DILATION * col_tap, rows, cols)
            before = before + jnp.einsum(
                "io,ihw->ohw", kernel[row_tap, col_tap], piece, preferred_element_type=jnp.float32
            )
    hidden = jnp.maximum(before, 0.0).astype(jnp.bfloat16)
    mixed = jnp.einsum("io,ihw->ohw", mixing, hidden, preferred_element_type=jnp.float32).astype(
        jnp.bfloat16
    )
    mixed_turned = mirror_tile(mixed)
    grad_turned = mirror_tile(cotangent)
    output = (
        maps.astype(jnp.float32)
        + 0.5 * (mixed.astype(jnp.float32) + mixed_turned.astype(jnp.float32))
    ).astype(jnp.bfloat16)
    grad_wide = cotangent.astype(jnp.float32)
    grad_mixed = (0.5 * (grad_wide + grad_turned.astype(jnp.float32))).astype(jnp.bfloat16)
    local_mixing = jnp.einsum("ihw,ohw->io", hidden, grad_mixed, preferred_element_type=jnp.float32)
    grad_hidden = jnp.einsum("io,ohw->ihw", mixing, grad_mixed, preferred_element_type=jnp.float32)
    grad_before = jnp.where(hidden > 0, grad_hidden, 0.0).astype(jnp.bfloat16)
    tap_grads = []
    for row_tap in range(3):
        for col_tap in range(3):
            piece = window(padded, DILATION * row_tap, DILATION * col_tap, rows, cols)
            tap_grads.append(
                jnp.einsum("ihw,ohw->io", piece, grad_before, preferred_element_type=jnp.float32)
            )
    local_kernel = jnp.stack(tap_grads).reshape(3, 3, chans, chans)
    flat = jnp.concatenate([local_kernel.reshape(-1), local_mixing.reshape(-1)])
    sums = all_sum(flat.reshape(-1, 128)).reshape(-1)
    grad_kernel = sums[: 9 * chans * chans].reshape(3, 3, chans, chans)
    grad_mixing = sums[9 * chans * chans :].reshape(chans, chans)
    grad_padded = with_halo(grad_before, (("row", 1), ("col", 2)), DILATION)
    grad_active = jnp.zeros((chans, rows, cols), jnp.float32)
    for row_tap in range(3):
        for col_tap in range(3):
            piece = window(
                grad_padded,
                2 * DILATION - DILATION * row_tap,
                2 * DILATION - DILATION * col_tap,
                rows,
                cols,
            )
            grad_active = grad_active + jnp.einsum(
                "io,ohw->ihw", kernel[row_tap, col_tap], piece, preferred_element_type=jnp.float32
            )
    grad_maps = (grad_wide + jnp.where(maps > 0, grad_active, 0.0)).astype(jnp.bfloat16)
    return (output, grad_maps, grad_kernel / map_bins, grad_mixing / map_bins)


def solution(mesh):
    placed = (P(None, "row", "col"), P(), P(), P(None, "row", "col"))
    return jax.shard_map(
        shards,
        mesh=mesh,
        in_specs=placed,
        out_specs=(P(None, "row", "col"), P(None, "row", "col"), P(), P()),
        check_vma=False,
    )
```

```python
import functools

import jax
import jax.numpy as jnp
from jax import lax
from jax.experimental import pallas as pl
from jax.experimental.pallas import tpu as pltpu
from jax.sharding import PartitionSpec as P

DILATION = 8


def with_halo(array, sides, width):
    for axis, dim in sides:
        peers, length = (lax.axis_size(axis), array.shape[dim])
        up = [(i, (i + 1) % peers) for i in range(peers - 1)]
        down = [(j, i) for i, j in up]
        last = lax.slice_in_dim(array, length - width, length, axis=dim)
        initial = lax.slice_in_dim(array, 0, width, axis=dim)
        before = lax.ppermute(last, axis, up)
        after = lax.ppermute(initial, axis, down)
        array = jnp.concatenate([before, array, after], axis=dim)
    return array


def flip(index, stride):
    return index + stride - 2 * stride * ((index // stride) % 2)


def sum_kernel(strides, x_ref, out_ref, arrived, partial, send_sem, recv_sem):
    row, col = lax.axis_index("row"), lax.axis_index("col")
    partners = [(flip(row, stride), col) if axis == "row" else (row, flip(col, stride)) for axis, stride in strides]
    barrier = pltpu.get_barrier_semaphore()
    for partner in partners:
        pl.semaphore_signal(barrier, inc=1, device_id=partner, device_id_type=pl.DeviceIdType.MESH)
    pl.semaphore_wait(barrier, len(partners))
    source = x_ref
    for step, partner in enumerate(partners):
        copy = pltpu.make_async_remote_copy(
            src_ref=source,
            dst_ref=arrived.at[step],
            send_sem=send_sem.at[step],
            recv_sem=recv_sem.at[step],
            device_id=partner,
            device_id_type=pl.DeviceIdType.MESH,
        )
        copy.start()
        copy.wait()
        target = out_ref if step == len(partners) - 1 else partial.at[step]
        target[...] = source[...] + arrived[step]
        source = target


def all_sum(x):
    strides = []
    for axis in ("row", "col"):
        peers = lax.axis_size(axis)
        stride = 1
        while stride < peers:
            strides.append((axis, stride))
            stride *= 2
    count = len(strides)
    return pl.pallas_call(
        functools.partial(sum_kernel, strides),
        out_shape=jax.ShapeDtypeStruct(x.shape, x.dtype),
        in_specs=[pl.BlockSpec(memory_space=pltpu.VMEM)],
        out_specs=pl.BlockSpec(memory_space=pltpu.VMEM),
        scratch_shapes=[
            pltpu.VMEM((count,) + x.shape, x.dtype),
            pltpu.VMEM((count,) + x.shape, x.dtype),
            pltpu.SemaphoreType.DMA((count,)),
            pltpu.SemaphoreType.DMA((count,)),
        ],
        compiler_params=pltpu.CompilerParams(collective_id=0, has_side_effects=True),
    )(x)


def mirror_tile(tile):
    row_count = lax.axis_size("row")
    col_count = lax.axis_size("col")
    chans, rows, cols = tile.shape
    group = cols // rows
    turn = lax.axis_index("row") % group
    pieces = jnp.roll(tile.reshape(chans, rows, group, rows), -turn, axis=2)
    landed = []
    for k in range(group):
        piece = jnp.swapaxes(pieces[:, :, k, :], 1, 2).reshape(chans, rows * rows)
        pairs = []
        for source_row in range(row_count):
            for source_col in range(col_count):
                target_row = group * source_col + (source_row % group + k) % group
                target = target_row * col_count + source_row // group
                pairs.append((source_row * col_count + source_col, target))
        landed.append(lax.ppermute(piece, ("row", "col"), pairs).reshape(chans, rows, rows))
    slots = jnp.stack([landed[(-i) % group] for i in range(group)], axis=2)
    return jnp.roll(slots, turn, axis=2).reshape(chans, rows, cols)


def window(padded, top, left, rows, cols):
    return padded[:, top : top + rows, left : left + cols]


def shards(maps, kernel, mixing, cotangent):
    chans, rows, cols = maps.shape
    map_bins = rows * lax.axis_size("row")
    active = jnp.maximum(maps, 0)
    padded = with_halo(active, (("row", 1), ("col", 2)), DILATION)
    before = jnp.zeros((chans, rows, cols), jnp.float32)
    for row_tap in range(3):
        for col_tap in range(3):
            piece = window(padded, DILATION * row_tap, DILATION * col_tap, rows, cols)
            before = before + jnp.einsum(
                "io,ihw->ohw", kernel[row_tap, col_tap], piece, preferred_element_type=jnp.float32
            )
    hidden = jnp.maximum(before, 0.0).astype(jnp.bfloat16)
    mixed = jnp.einsum("io,ihw->ohw", mixing, hidden, preferred_element_type=jnp.float32).astype(
        jnp.bfloat16
    )
    grad_turned = mirror_tile(cotangent)
    grad_wide = cotangent.astype(jnp.float32)
    grad_mixed = (0.5 * (grad_wide + grad_turned.astype(jnp.float32))).astype(jnp.bfloat16)
    local_mixing = jnp.einsum("ihw,ohw->io", hidden, grad_mixed, preferred_element_type=jnp.float32)
    grad_hidden = jnp.einsum("io,ohw->ihw", mixing, grad_mixed, preferred_element_type=jnp.float32)
    grad_before = jnp.where(hidden > 0, grad_hidden, 0.0).astype(jnp.bfloat16)
    tap_grads = []
    for row_tap in range(3):
        for col_tap in range(3):
            piece = window(padded, DILATION * row_tap, DILATION * col_tap, rows, cols)
            tap_grads.append(
                jnp.einsum("ihw,ohw->io", piece, grad_before, preferred_element_type=jnp.float32)
            )
    local_kernel = jnp.stack(tap_grads).reshape(3, 3, chans, chans)
    flat = jnp.concatenate([local_kernel.reshape(-1), local_mixing.reshape(-1)])
    sums = all_sum(flat.reshape(-1, 128)).reshape(-1)
    sums, mixed = lax.optimization_barrier((sums, mixed))
    grad_kernel = sums[: 9 * chans * chans].reshape(3, 3, chans, chans)
    grad_mixing = sums[9 * chans * chans :].reshape(chans, chans)
    mixed_turned = mirror_tile(mixed)
    output = (
        maps.astype(jnp.float32)
        + 0.5 * (mixed.astype(jnp.float32) + mixed_turned.astype(jnp.float32))
    ).astype(jnp.bfloat16)
    grad_padded = with_halo(grad_before, (("row", 1), ("col", 2)), DILATION)
    grad_active = jnp.zeros((chans, rows, cols), jnp.float32)
    for row_tap in range(3):
        for col_tap in range(3):
            piece = window(
                grad_padded,
                2 * DILATION - DILATION * row_tap,
                2 * DILATION - DILATION * col_tap,
                rows,
                cols,
            )
            grad_active = grad_active + jnp.einsum(
                "io,ohw->ihw", kernel[row_tap, col_tap], piece, preferred_element_type=jnp.float32
            )
    grad_maps = (grad_wide + jnp.where(maps > 0, grad_active, 0.0)).astype(jnp.bfloat16)
    return (output, grad_maps, grad_kernel / map_bins, grad_mixing / map_bins)


def solution(mesh):
    placed = (P(None, "row", "col"), P(), P(), P(None, "row", "col"))
    return jax.shard_map(
        shards,
        mesh=mesh,
        in_specs=placed,
        out_specs=(P(None, "row", "col"), P(None, "row", "col"), P(), P()),
        check_vma=False,
    )
```

```python
import jax
import jax.numpy as jnp
from jax import lax
from jax.sharding import PartitionSpec as P

DILATION = 8


def with_halo(array, sides, width):
    for axis, dim in sides:
        peers, length = (lax.axis_size(axis), array.shape[dim])
        up = [(i, (i + 1) % peers) for i in range(peers - 1)]
        down = [(j, i) for i, j in up]
        last = lax.slice_in_dim(array, length - width, length, axis=dim)
        initial = lax.slice_in_dim(array, 0, width, axis=dim)
        before = lax.ppermute(last, axis, up)
        after = lax.ppermute(initial, axis, down)
        array = jnp.concatenate([before, array, after], axis=dim)
    return array


def all_sum(x, axes):
    for axis in axes:
        peers = lax.axis_size(axis)
        if peers & (peers - 1):
            x = lax.psum(x, axis)
            continue
        step = 1
        while step < peers:
            x = x + lax.ppermute(x, axis, [(i, i ^ step) for i in range(peers)])
            step *= 2
    return x


def mirror_tile(tile):
    row_count = lax.axis_size("row")
    col_count = lax.axis_size("col")
    chans, rows, cols = tile.shape
    group = cols // rows
    turn = lax.axis_index("row") % group
    pieces = jnp.roll(tile.reshape(chans, rows, group, rows), -turn, axis=2)
    landed = []
    for k in range(group):
        piece = jnp.swapaxes(pieces[:, :, k, :], 1, 2).reshape(chans, rows * rows)
        pairs = []
        for source_row in range(row_count):
            for source_col in range(col_count):
                target_row = group * source_col + (source_row % group + k) % group
                target = target_row * col_count + source_row // group
                pairs.append((source_row * col_count + source_col, target))
        landed.append(lax.ppermute(piece, ("row", "col"), pairs).reshape(chans, rows, rows))
    slots = jnp.stack([landed[(-i) % group] for i in range(group)], axis=2)
    return jnp.roll(slots, turn, axis=2).reshape(chans, rows, cols)


def window(padded, top, left, rows, cols):
    return padded[:, top : top + rows, left : left + cols]


def shards(maps, kernel, mixing, cotangent):
    chans, rows, cols = maps.shape
    map_bins = rows * lax.axis_size("row")
    active = jnp.maximum(maps, 0)
    padded = with_halo(active, (("row", 1), ("col", 2)), DILATION)
    before = jnp.zeros((chans, rows, cols), jnp.float32)
    for row_tap in range(3):
        for col_tap in range(3):
            piece = window(padded, DILATION * row_tap, DILATION * col_tap, rows, cols)
            before = before + jnp.einsum(
                "io,ihw->ohw", kernel[row_tap, col_tap], piece, preferred_element_type=jnp.float32
            )
    hidden = jnp.maximum(before, 0.0).astype(jnp.bfloat16)
    mixed = jnp.einsum("io,ihw->ohw", mixing, hidden, preferred_element_type=jnp.float32).astype(
        jnp.bfloat16
    )
    turned = mirror_tile(jnp.concatenate([cotangent, mixed]))
    grad_turned, mixed_turned = turned[:chans], turned[chans:]
    output = (
        maps.astype(jnp.float32)
        + 0.5 * (mixed.astype(jnp.float32) + mixed_turned.astype(jnp.float32))
    ).astype(jnp.bfloat16)
    grad_wide = cotangent.astype(jnp.float32)
    grad_mixed = (0.5 * (grad_wide + grad_turned.astype(jnp.float32))).astype(jnp.bfloat16)
    local_mixing = jnp.einsum("ihw,ohw->io", hidden, grad_mixed, preferred_element_type=jnp.float32)
    grad_hidden = jnp.einsum("io,ohw->ihw", mixing, grad_mixed, preferred_element_type=jnp.float32)
    grad_before = jnp.where(hidden > 0, grad_hidden, 0.0).astype(jnp.bfloat16)
    tap_grads = []
    for row_tap in range(3):
        for col_tap in range(3):
            piece = window(padded, DILATION * row_tap, DILATION * col_tap, rows, cols)
            tap_grads.append(
                jnp.einsum("ihw,ohw->io", piece, grad_before, preferred_element_type=jnp.float32)
            )
    local_kernel = jnp.stack(tap_grads).reshape(3, 3, chans, chans)
    flat = jnp.concatenate([local_kernel.reshape(-1), local_mixing.reshape(-1)])
    sums = all_sum(flat.reshape(-1, 128), ("row", "col")).reshape(-1)
    grad_kernel = sums[: 9 * chans * chans].reshape(3, 3, chans, chans)
    grad_mixing = sums[9 * chans * chans :].reshape(chans, chans)
    grad_padded = with_halo(grad_before, (("row", 1), ("col", 2)), DILATION)
    grad_active = jnp.zeros((chans, rows, cols), jnp.float32)
    for row_tap in range(3):
        for col_tap in range(3):
            piece = window(
                grad_padded,
                2 * DILATION - DILATION * row_tap,
                2 * DILATION - DILATION * col_tap,
                rows,
                cols,
            )
            grad_active = grad_active + jnp.einsum(
                "io,ohw->ihw", kernel[row_tap, col_tap], piece, preferred_element_type=jnp.float32
            )
    grad_maps = (grad_wide + jnp.where(maps > 0, grad_active, 0.0)).astype(jnp.bfloat16)
    return (output, grad_maps, grad_kernel / map_bins, grad_mixing / map_bins)


def solution(mesh):
    placed = (P(None, "row", "col"), P(), P(), P(None, "row", "col"))
    return jax.shard_map(
        shards,
        mesh=mesh,
        in_specs=placed,
        out_specs=(P(None, "row", "col"), P(None, "row", "col"), P(), P()),
        check_vma=False,
    )
```

```python
import jax
import jax.numpy as jnp
from jax import lax
from jax.sharding import PartitionSpec as P

DILATION = 8


def with_halo(array, sides, width):
    for axis, dim in sides:
        peers, length = (lax.axis_size(axis), array.shape[dim])
        up = [(i, (i + 1) % peers) for i in range(peers - 1)]
        down = [(j, i) for i, j in up]
        last = lax.slice_in_dim(array, length - width, length, axis=dim)
        initial = lax.slice_in_dim(array, 0, width, axis=dim)
        before = lax.ppermute(last, axis, up)
        after = lax.ppermute(initial, axis, down)
        array = jnp.concatenate([before, array, after], axis=dim)
    return array


def all_sum(x, axes):
    for axis in axes:
        peers = lax.axis_size(axis)
        if peers & (peers - 1):
            x = lax.psum(x, axis)
            continue
        step = 1
        while step < peers:
            x = x + lax.ppermute(x, axis, [(i, i ^ step) for i in range(peers)])
            step *= 2
    return x


def mirror_tile(tile):
    row_count = lax.axis_size("row")
    col_count = lax.axis_size("col")
    chans, rows, cols = tile.shape
    group = cols // rows
    turn = lax.axis_index("row") % group
    pieces = jnp.roll(tile.reshape(chans, rows, group, rows), -turn, axis=2)
    landed = []
    for k in range(group):
        piece = jnp.swapaxes(pieces[:, :, k, :], 1, 2).reshape(chans, rows * rows)
        pairs = []
        for source_row in range(row_count):
            for source_col in range(col_count):
                target_row = group * source_col + (source_row % group + k) % group
                target = target_row * col_count + source_row // group
                pairs.append((source_row * col_count + source_col, target))
        landed.append(lax.ppermute(piece, ("row", "col"), pairs).reshape(chans, rows, rows))
    slots = jnp.stack([landed[(-i) % group] for i in range(group)], axis=2)
    return jnp.roll(slots, turn, axis=2).reshape(chans, rows, cols)


def window(padded, top, left, rows, cols):
    return padded[:, top : top + rows, left : left + cols]


def shards(maps, kernel, mixing, cotangent):
    chans, rows, cols = maps.shape
    map_bins = rows * lax.axis_size("row")
    active = jnp.maximum(maps, 0)
    padded = with_halo(active, (("row", 1), ("col", 2)), DILATION)
    before = jnp.zeros((chans, rows, cols), jnp.float32)
    for row_tap in range(3):
        for col_tap in range(3):
            piece = window(padded, DILATION * row_tap, DILATION * col_tap, rows, cols)
            before = before + jnp.einsum(
                "io,ihw->ohw", kernel[row_tap, col_tap], piece, preferred_element_type=jnp.float32
            )
    hidden = jnp.maximum(before, 0.0).astype(jnp.bfloat16)
    mixed = jnp.einsum("io,ihw->ohw", mixing, hidden, preferred_element_type=jnp.float32).astype(
        jnp.bfloat16
    )
    grad_turned = mirror_tile(cotangent)
    grad_wide = cotangent.astype(jnp.float32)
    grad_mixed = (0.5 * (grad_wide + grad_turned.astype(jnp.float32))).astype(jnp.bfloat16)
    local_mixing = jnp.einsum("ihw,ohw->io", hidden, grad_mixed, preferred_element_type=jnp.float32)
    grad_hidden = jnp.einsum("io,ohw->ihw", mixing, grad_mixed, preferred_element_type=jnp.float32)
    grad_before = jnp.where(hidden > 0, grad_hidden, 0.0).astype(jnp.bfloat16)
    tap_grads = []
    for row_tap in range(3):
        for col_tap in range(3):
            piece = window(padded, DILATION * row_tap, DILATION * col_tap, rows, cols)
            tap_grads.append(
                jnp.einsum("ihw,ohw->io", piece, grad_before, preferred_element_type=jnp.float32)
            )
    local_kernel = jnp.stack(tap_grads).reshape(3, 3, chans, chans)
    flat = jnp.concatenate([local_kernel.reshape(-1), local_mixing.reshape(-1)])
    flat, mixed = lax.optimization_barrier((flat, mixed))
    mixed_turned = mirror_tile(mixed)
    output = (
        maps.astype(jnp.float32)
        + 0.5 * (mixed.astype(jnp.float32) + mixed_turned.astype(jnp.float32))
    ).astype(jnp.bfloat16)
    sums = all_sum(flat.reshape(-1, 128), ("row", "col")).reshape(-1)
    grad_kernel = sums[: 9 * chans * chans].reshape(3, 3, chans, chans)
    grad_mixing = sums[9 * chans * chans :].reshape(chans, chans)
    grad_padded = with_halo(grad_before, (("row", 1), ("col", 2)), DILATION)
    grad_active = jnp.zeros((chans, rows, cols), jnp.float32)
    for row_tap in range(3):
        for col_tap in range(3):
            piece = window(
                grad_padded,
                2 * DILATION - DILATION * row_tap,
                2 * DILATION - DILATION * col_tap,
                rows,
                cols,
            )
            grad_active = grad_active + jnp.einsum(
                "io,ohw->ihw", kernel[row_tap, col_tap], piece, preferred_element_type=jnp.float32
            )
    grad_maps = (grad_wide + jnp.where(maps > 0, grad_active, 0.0)).astype(jnp.bfloat16)
    return (output, grad_maps, grad_kernel / map_bins, grad_mixing / map_bins)


def solution(mesh):
    placed = (P(None, "row", "col"), P(), P(), P(None, "row", "col"))
    return jax.shard_map(
        shards,
        mesh=mesh,
        in_specs=placed,
        out_specs=(P(None, "row", "col"), P(None, "row", "col"), P(), P()),
        check_vma=False,
    )
```

```python
import functools

import jax
import jax.numpy as jnp
from jax import lax
from jax.experimental import pallas as pl
from jax.experimental.pallas import tpu as pltpu
from jax.sharding import PartitionSpec as P

DILATION = 8


def with_halo(array, sides, width):
    for axis, dim in sides:
        peers, length = (lax.axis_size(axis), array.shape[dim])
        up = [(i, (i + 1) % peers) for i in range(peers - 1)]
        down = [(j, i) for i, j in up]
        last = lax.slice_in_dim(array, length - width, length, axis=dim)
        initial = lax.slice_in_dim(array, 0, width, axis=dim)
        before = lax.ppermute(last, axis, up)
        after = lax.ppermute(initial, axis, down)
        array = jnp.concatenate([before, array, after], axis=dim)
    return array


def flip(index, stride):
    return index + stride - 2 * stride * ((index // stride) % 2)


def sum_kernel(strides, x_ref, out_ref, arrived, partial, send_sem, recv_sem):
    row, col = lax.axis_index("row"), lax.axis_index("col")
    partners = [(flip(row, stride), col) if axis == "row" else (row, flip(col, stride)) for axis, stride in strides]
    barrier = pltpu.get_barrier_semaphore()
    for partner in partners:
        pl.semaphore_signal(barrier, inc=1, device_id=partner, device_id_type=pl.DeviceIdType.MESH)
    pl.semaphore_wait(barrier, len(partners))
    source = x_ref
    for step, partner in enumerate(partners):
        copy = pltpu.make_async_remote_copy(
            src_ref=source,
            dst_ref=arrived.at[step],
            send_sem=send_sem.at[step],
            recv_sem=recv_sem.at[step],
            device_id=partner,
            device_id_type=pl.DeviceIdType.MESH,
        )
        copy.start()
        copy.wait()
        target = out_ref if step == len(partners) - 1 else partial.at[step]
        target[...] = source[...] + arrived[step]
        source = target


def all_sum(x):
    strides = []
    for axis in ("row", "col"):
        peers = lax.axis_size(axis)
        stride = 1
        while stride < peers:
            strides.append((axis, stride))
            stride *= 2
    count = len(strides)
    return pl.pallas_call(
        functools.partial(sum_kernel, strides),
        out_shape=jax.ShapeDtypeStruct(x.shape, x.dtype),
        in_specs=[pl.BlockSpec(memory_space=pltpu.VMEM)],
        out_specs=pl.BlockSpec(memory_space=pltpu.VMEM),
        scratch_shapes=[
            pltpu.VMEM((count,) + x.shape, x.dtype),
            pltpu.VMEM((count,) + x.shape, x.dtype),
            pltpu.SemaphoreType.DMA((count,)),
            pltpu.SemaphoreType.DMA((count,)),
        ],
        compiler_params=pltpu.CompilerParams(collective_id=0, has_side_effects=True),
    )(x)


def mirror_tile(tile):
    row_count = lax.axis_size("row")
    col_count = lax.axis_size("col")
    chans, rows, cols = tile.shape
    group = cols // rows
    turn = lax.axis_index("row") % group
    pieces = jnp.roll(tile.reshape(chans, rows, group, rows), -turn, axis=2)
    landed = []
    for k in range(group):
        piece = jnp.swapaxes(pieces[:, :, k, :], 1, 2).reshape(chans, rows * rows)
        pairs = []
        for source_row in range(row_count):
            for source_col in range(col_count):
                target_row = group * source_col + (source_row % group + k) % group
                target = target_row * col_count + source_row // group
                pairs.append((source_row * col_count + source_col, target))
        landed.append(lax.ppermute(piece, ("row", "col"), pairs).reshape(chans, rows, rows))
    slots = jnp.stack([landed[(-i) % group] for i in range(group)], axis=2)
    return jnp.roll(slots, turn, axis=2).reshape(chans, rows, cols)


def window(padded, top, left, rows, cols):
    return padded[:, top : top + rows, left : left + cols]


def shards(maps, kernel, mixing, cotangent):
    chans, rows, cols = maps.shape
    map_bins = rows * lax.axis_size("row")
    active = jnp.maximum(maps, 0)
    padded = with_halo(active, (("row", 1), ("col", 2)), DILATION)
    before = jnp.zeros((chans, rows, cols), jnp.float32)
    for row_tap in range(3):
        for col_tap in range(3):
            piece = window(padded, DILATION * row_tap, DILATION * col_tap, rows, cols)
            before = before + jnp.einsum(
                "io,ihw->ohw", kernel[row_tap, col_tap], piece, preferred_element_type=jnp.float32
            )
    hidden = jnp.maximum(before, 0.0).astype(jnp.bfloat16)
    mixed = jnp.einsum("io,ihw->ohw", mixing, hidden, preferred_element_type=jnp.float32).astype(
        jnp.bfloat16
    )
    mixed_turned = mirror_tile(mixed)
    grad_turned = mirror_tile(cotangent)
    output = (
        maps.astype(jnp.float32)
        + 0.5 * (mixed.astype(jnp.float32) + mixed_turned.astype(jnp.float32))
    ).astype(jnp.bfloat16)
    grad_wide = cotangent.astype(jnp.float32)
    grad_mixed = (0.5 * (grad_wide + grad_turned.astype(jnp.float32))).astype(jnp.bfloat16)
    local_mixing = jnp.einsum("ihw,ohw->io", hidden, grad_mixed, preferred_element_type=jnp.float32)
    grad_hidden = jnp.einsum("io,ohw->ihw", mixing, grad_mixed, preferred_element_type=jnp.float32)
    grad_before = jnp.where(hidden > 0, grad_hidden, 0.0).astype(jnp.bfloat16)
    tap_grads = []
    for row_tap in range(3):
        for col_tap in range(3):
            piece = window(padded, DILATION * row_tap, DILATION * col_tap, rows, cols)
            tap_grads.append(
                jnp.einsum("ihw,ohw->io", piece, grad_before, preferred_element_type=jnp.float32)
            )
    local_kernel = jnp.stack(tap_grads).reshape(3, 3, chans, chans)
    flat = jnp.concatenate([local_kernel.reshape(-1), local_mixing.reshape(-1)])
    grad_padded = with_halo(grad_before, (("row", 1), ("col", 2)), DILATION)
    grad_active = jnp.zeros((chans, rows, cols), jnp.float32)
    for row_tap in range(3):
        for col_tap in range(3):
            piece = window(
                grad_padded,
                2 * DILATION - DILATION * row_tap,
                2 * DILATION - DILATION * col_tap,
                rows,
                cols,
            )
            grad_active = grad_active + jnp.einsum(
                "io,ohw->ihw", kernel[row_tap, col_tap], piece, preferred_element_type=jnp.float32
            )
    grad_maps = (grad_wide + jnp.where(maps > 0, grad_active, 0.0)).astype(jnp.bfloat16)
    flat, output, grad_maps = lax.optimization_barrier((flat, output, grad_maps))
    sums = all_sum(flat.reshape(-1, 128)).reshape(-1)
    grad_kernel = sums[: 9 * chans * chans].reshape(3, 3, chans, chans)
    grad_mixing = sums[9 * chans * chans :].reshape(chans, chans)
    return (output, grad_maps, grad_kernel / map_bins, grad_mixing / map_bins)


def solution(mesh):
    placed = (P(None, "row", "col"), P(), P(), P(None, "row", "col"))
    return jax.shard_map(
        shards,
        mesh=mesh,
        in_specs=placed,
        out_specs=(P(None, "row", "col"), P(None, "row", "col"), P(), P()),
        check_vma=False,
    )
```

```python
import jax
import jax.numpy as jnp
from jax import lax
from jax.sharding import PartitionSpec as P

DILATION = 8


def with_halo(array, sides, width):
    for axis, dim in sides:
        peers, length = (lax.axis_size(axis), array.shape[dim])
        up = [(i, (i + 1) % peers) for i in range(peers - 1)]
        down = [(j, i) for i, j in up]
        last = lax.slice_in_dim(array, length - width, length, axis=dim)
        initial = lax.slice_in_dim(array, 0, width, axis=dim)
        before = lax.ppermute(last, axis, up)
        after = lax.ppermute(initial, axis, down)
        array = jnp.concatenate([before, array, after], axis=dim)
    return array


RING_DIGITS = {"row": (2, 8, 2), "col": (4, 2)}


def gray(value):
    return value ^ (value >> 1)


def gray_inverse(value):
    result = 0
    while value:
        result ^= value
        value >>= 1
    return result


def ring_partner(index, digits, digit, bit):
    place = 1
    for size in digits[digit + 1 :]:
        place *= size
    value = index // place % digits[digit]
    flipped = gray(gray_inverse(value) ^ (1 << bit))
    return index + (flipped - value) * place


def all_sum(x, axes):
    for axis in axes:
        peers = lax.axis_size(axis)
        digits = RING_DIGITS.get(axis, (peers,))
        product = 1
        for size in digits:
            product *= size
        if product != peers or any(size & (size - 1) for size in digits):
            x = lax.psum(x, axis)
            continue
        for digit in reversed(range(len(digits))):
            for bit in range(digits[digit].bit_length() - 1):
                pairs = [(i, ring_partner(i, digits, digit, bit)) for i in range(peers)]
                x = x + lax.ppermute(x, axis, pairs)
    return x


def mirror_tile(tile):
    row_count = lax.axis_size("row")
    col_count = lax.axis_size("col")
    chans, rows, cols = tile.shape
    width = rows // col_count
    strip = lax.all_to_all(tile, "col", split_axis=1, concat_axis=2, tiled=True)
    blocks = lax.all_to_all(strip, "row", split_axis=2, concat_axis=1, tiled=True)
    turned = jnp.transpose(blocks.reshape(chans, row_count, width, rows), (0, 3, 1, 2))
    landed = lax.all_to_all(turned, "col", split_axis=2, concat_axis=3, tiled=True)
    return landed.reshape(chans, rows, cols)


def window(padded, top, left, rows, cols):
    return padded[:, top : top + rows, left : left + cols]


def shards(maps, kernel, mixing, cotangent):
    chans, rows, cols = maps.shape
    map_bins = rows * lax.axis_size("row")
    active = jnp.maximum(maps, 0)
    padded = with_halo(active, (("row", 1), ("col", 2)), DILATION)
    before = jnp.zeros((chans, rows, cols), jnp.float32)
    for row_tap in range(3):
        for col_tap in range(3):
            piece = window(padded, DILATION * row_tap, DILATION * col_tap, rows, cols)
            before = before + jnp.einsum(
                "io,ihw->ohw", kernel[row_tap, col_tap], piece, preferred_element_type=jnp.float32
            )
    hidden = jnp.maximum(before, 0.0).astype(jnp.bfloat16)
    mixed = jnp.einsum("io,ihw->ohw", mixing, hidden, preferred_element_type=jnp.float32).astype(
        jnp.bfloat16
    )
    mixed_turned = mirror_tile(mixed)
    grad_turned = mirror_tile(cotangent)
    output = (
        maps.astype(jnp.float32)
        + 0.5 * (mixed.astype(jnp.float32) + mixed_turned.astype(jnp.float32))
    ).astype(jnp.bfloat16)
    grad_wide = cotangent.astype(jnp.float32)
    grad_mixed = (0.5 * (grad_wide + grad_turned.astype(jnp.float32))).astype(jnp.bfloat16)
    local_mixing = jnp.einsum("ihw,ohw->io", hidden, grad_mixed, preferred_element_type=jnp.float32)
    grad_hidden = jnp.einsum("io,ohw->ihw", mixing, grad_mixed, preferred_element_type=jnp.float32)
    grad_before = jnp.where(hidden > 0, grad_hidden, 0.0).astype(jnp.bfloat16)
    tap_grads = []
    for row_tap in range(3):
        for col_tap in range(3):
            piece = window(padded, DILATION * row_tap, DILATION * col_tap, rows, cols)
            tap_grads.append(
                jnp.einsum("ihw,ohw->io", piece, grad_before, preferred_element_type=jnp.float32)
            )
    local_kernel = jnp.stack(tap_grads).reshape(3, 3, chans, chans)
    flat = jnp.concatenate([local_kernel.reshape(-1), local_mixing.reshape(-1)])
    sums = all_sum(flat.reshape(-1, 128), ("row", "col")).reshape(-1)
    grad_kernel = sums[: 9 * chans * chans].reshape(3, 3, chans, chans)
    grad_mixing = sums[9 * chans * chans :].reshape(chans, chans)
    grad_padded = with_halo(grad_before, (("row", 1), ("col", 2)), DILATION)
    grad_active = jnp.zeros((chans, rows, cols), jnp.float32)
    for row_tap in range(3):
        for col_tap in range(3):
            piece = window(
                grad_padded,
                2 * DILATION - DILATION * row_tap,
                2 * DILATION - DILATION * col_tap,
                rows,
                cols,
            )
            grad_active = grad_active + jnp.einsum(
                "io,ohw->ihw", kernel[row_tap, col_tap], piece, preferred_element_type=jnp.float32
            )
    grad_maps = (grad_wide + jnp.where(maps > 0, grad_active, 0.0)).astype(jnp.bfloat16)
    return (output, grad_maps, grad_kernel / map_bins, grad_mixing / map_bins)


def solution(mesh):
    placed = (P(None, "row", "col"), P(), P(), P(None, "row", "col"))
    return jax.shard_map(
        shards,
        mesh=mesh,
        in_specs=placed,
        out_specs=(P(None, "row", "col"), P(None, "row", "col"), P(), P()),
        check_vma=False,
    )
```

```python
import jax
import jax.numpy as jnp
from jax import lax
from jax.sharding import PartitionSpec as P

DILATION = 8


def with_halo(array, sides, width):
    for axis, dim in sides:
        peers, length = (lax.axis_size(axis), array.shape[dim])
        up = [(i, (i + 1) % peers) for i in range(peers - 1)]
        down = [(j, i) for i, j in up]
        last = lax.slice_in_dim(array, length - width, length, axis=dim)
        initial = lax.slice_in_dim(array, 0, width, axis=dim)
        before = lax.ppermute(last, axis, up)
        after = lax.ppermute(initial, axis, down)
        array = jnp.concatenate([before, array, after], axis=dim)
    return array


RING_DIGITS = {"row": (2, 8, 2), "col": (4, 2)}


def gray(value):
    return value ^ (value >> 1)


def gray_inverse(value):
    result = 0
    while value:
        result ^= value
        value >>= 1
    return result


def ring_partner(index, digits, digit, bit):
    place = 1
    for size in digits[digit + 1 :]:
        place *= size
    value = index // place % digits[digit]
    flipped = gray(gray_inverse(value) ^ (1 << bit))
    return index + (flipped - value) * place


def all_sum(x, axes):
    for axis in axes:
        peers = lax.axis_size(axis)
        digits = RING_DIGITS.get(axis, (peers,))
        product = 1
        for size in digits:
            product *= size
        if product != peers or any(size & (size - 1) for size in digits):
            x = lax.psum(x, axis)
            continue
        for digit in reversed(range(len(digits))):
            for bit in range(digits[digit].bit_length() - 1):
                pairs = [(i, ring_partner(i, digits, digit, bit)) for i in range(peers)]
                x = x + lax.ppermute(x, axis, pairs)
    return x


def mirror_tile(tile):
    row_count = lax.axis_size("row")
    col_count = lax.axis_size("col")
    chans, rows, cols = tile.shape
    width = rows // col_count
    strip = lax.all_to_all(tile, "col", split_axis=1, concat_axis=2, tiled=True)
    blocks = lax.all_to_all(strip, "row", split_axis=2, concat_axis=1, tiled=True)
    turned = jnp.transpose(blocks.reshape(chans, row_count, width, rows), (0, 3, 1, 2))
    landed = lax.all_to_all(turned, "col", split_axis=2, concat_axis=3, tiled=True)
    return landed.reshape(chans, rows, cols)


def window(padded, top, left, rows, cols):
    return padded[:, top : top + rows, left : left + cols]


def shards(maps, kernel, mixing, cotangent):
    chans, rows, cols = maps.shape
    map_bins = rows * lax.axis_size("row")
    active = jnp.maximum(maps, 0)
    padded = with_halo(active, (("row", 1), ("col", 2)), DILATION)
    taps = kernel.reshape(9, chans, chans)
    pieces = jnp.stack(
        [window(padded, DILATION * a, DILATION * b, rows, cols) for a in range(3) for b in range(3)]
    )
    before = jnp.einsum("tio,tihw->ohw", taps, pieces, preferred_element_type=jnp.float32)
    hidden = jnp.maximum(before, 0.0).astype(jnp.bfloat16)
    mixed = jnp.einsum("io,ihw->ohw", mixing, hidden, preferred_element_type=jnp.float32).astype(
        jnp.bfloat16
    )
    mixed_turned = mirror_tile(mixed)
    grad_turned = mirror_tile(cotangent)
    output = (
        maps.astype(jnp.float32)
        + 0.5 * (mixed.astype(jnp.float32) + mixed_turned.astype(jnp.float32))
    ).astype(jnp.bfloat16)
    grad_wide = cotangent.astype(jnp.float32)
    grad_mixed = (0.5 * (grad_wide + grad_turned.astype(jnp.float32))).astype(jnp.bfloat16)
    local_mixing = jnp.einsum("ihw,ohw->io", hidden, grad_mixed, preferred_element_type=jnp.float32)
    grad_hidden = jnp.einsum("io,ohw->ihw", mixing, grad_mixed, preferred_element_type=jnp.float32)
    grad_before = jnp.where(hidden > 0, grad_hidden, 0.0).astype(jnp.bfloat16)
    local_kernel = jnp.einsum("tihw,ohw->tio", pieces, grad_before, preferred_element_type=jnp.float32)
    flat = jnp.concatenate([local_kernel.reshape(-1), local_mixing.reshape(-1)])
    sums = all_sum(flat.reshape(-1, 128), ("row", "col")).reshape(-1)
    grad_kernel = sums[: 9 * chans * chans].reshape(3, 3, chans, chans)
    grad_mixing = sums[9 * chans * chans :].reshape(chans, chans)
    grad_padded = with_halo(grad_before, (("row", 1), ("col", 2)), DILATION)
    grad_pieces = jnp.stack(
        [
            window(grad_padded, 2 * DILATION - DILATION * a, 2 * DILATION - DILATION * b, rows, cols)
            for a in range(3)
            for b in range(3)
        ]
    )
    grad_active = jnp.einsum("tio,tohw->ihw", taps, grad_pieces, preferred_element_type=jnp.float32)
    grad_maps = (grad_wide + jnp.where(maps > 0, grad_active, 0.0)).astype(jnp.bfloat16)
    return (output, grad_maps, grad_kernel / map_bins, grad_mixing / map_bins)


def solution(mesh):
    placed = (P(None, "row", "col"), P(), P(), P(None, "row", "col"))
    return jax.shard_map(
        shards,
        mesh=mesh,
        in_specs=placed,
        out_specs=(P(None, "row", "col"), P(None, "row", "col"), P(), P()),
        check_vma=False,
    )
```

```python
import jax
import jax.numpy as jnp
from jax import lax
from jax.sharding import PartitionSpec as P

DILATION = 8


def with_halo(array, sides, width):
    for axis, dim in sides:
        peers, length = (lax.axis_size(axis), array.shape[dim])
        up = [(i, (i + 1) % peers) for i in range(peers - 1)]
        down = [(j, i) for i, j in up]
        last = lax.slice_in_dim(array, length - width, length, axis=dim)
        initial = lax.slice_in_dim(array, 0, width, axis=dim)
        before = lax.ppermute(last, axis, up)
        after = lax.ppermute(initial, axis, down)
        array = jnp.concatenate([before, array, after], axis=dim)
    return array


RING_DIGITS = {"row": (2, 8, 2), "col": (4, 2)}


def gray(value):
    return value ^ (value >> 1)


def gray_inverse(value):
    result = 0
    while value:
        result ^= value
        value >>= 1
    return result


def ring_partner(index, digits, digit, bit):
    place = 1
    for size in digits[digit + 1 :]:
        place *= size
    value = index // place % digits[digit]
    flipped = gray(gray_inverse(value) ^ (1 << bit))
    return index + (flipped - value) * place


def all_sum(x, axes):
    for axis in axes:
        peers = lax.axis_size(axis)
        digits = RING_DIGITS.get(axis, (peers,))
        product = 1
        for size in digits:
            product *= size
        if product != peers or any(size & (size - 1) for size in digits):
            x = lax.psum(x, axis)
            continue
        for digit in reversed(range(len(digits))):
            for bit in range(digits[digit].bit_length() - 1):
                pairs = [(i, ring_partner(i, digits, digit, bit)) for i in range(peers)]
                x = x + lax.ppermute(x, axis, pairs)
    return x


def mirror_tile(tile):
    row_count = lax.axis_size("row")
    col_count = lax.axis_size("col")
    chans, rows, cols = tile.shape
    group = cols // rows
    turn = lax.axis_index("row") % group
    pieces = jnp.roll(tile.reshape(chans, rows, group, rows), -turn, axis=2)
    landed = []
    for k in range(group):
        piece = jnp.swapaxes(pieces[:, :, k, :], 1, 2).reshape(chans, rows * rows)
        pairs = []
        for source_row in range(row_count):
            for source_col in range(col_count):
                target_row = group * source_col + (source_row % group + k) % group
                target = target_row * col_count + source_row // group
                pairs.append((source_row * col_count + source_col, target))
        landed.append(lax.ppermute(piece, ("row", "col"), pairs).reshape(chans, rows, rows))
    slots = jnp.stack([landed[(-i) % group] for i in range(group)], axis=2)
    return jnp.roll(slots, turn, axis=2).reshape(chans, rows, cols)


def window(padded, top, left, rows, cols):
    return padded[:, top : top + rows, left : left + cols]


def shards(maps, kernel, mixing, cotangent):
    chans, rows, cols = maps.shape
    map_bins = rows * lax.axis_size("row")
    active = jnp.maximum(maps, 0)
    padded = with_halo(active, (("row", 1), ("col", 2)), DILATION)
    taps = kernel.reshape(9, chans, chans)
    pieces = jnp.stack(
        [window(padded, DILATION * a, DILATION * b, rows, cols) for a in range(3) for b in range(3)]
    )
    before = jnp.einsum("tio,tihw->ohw", taps, pieces, preferred_element_type=jnp.float32)
    hidden = jnp.maximum(before, 0.0).astype(jnp.bfloat16)
    mixed = jnp.einsum("io,ihw->ohw", mixing, hidden, preferred_element_type=jnp.float32).astype(
        jnp.bfloat16
    )
    mixed_turned = mirror_tile(mixed)
    grad_turned = mirror_tile(cotangent)
    output = (
        maps.astype(jnp.float32)
        + 0.5 * (mixed.astype(jnp.float32) + mixed_turned.astype(jnp.float32))
    ).astype(jnp.bfloat16)
    grad_wide = cotangent.astype(jnp.float32)
    grad_mixed = (0.5 * (grad_wide + grad_turned.astype(jnp.float32))).astype(jnp.bfloat16)
    local_mixing = jnp.einsum("ihw,ohw->io", hidden, grad_mixed, preferred_element_type=jnp.float32)
    grad_hidden = jnp.einsum("io,ohw->ihw", mixing, grad_mixed, preferred_element_type=jnp.float32)
    grad_before = jnp.where(hidden > 0, grad_hidden, 0.0).astype(jnp.bfloat16)
    local_kernel = jnp.einsum("tihw,ohw->tio", pieces, grad_before, preferred_element_type=jnp.float32)
    flat = jnp.concatenate([local_kernel.reshape(-1), local_mixing.reshape(-1)])
    sums = all_sum(flat.reshape(-1, 128), ("row", "col")).reshape(-1)
    grad_kernel = sums[: 9 * chans * chans].reshape(3, 3, chans, chans)
    grad_mixing = sums[9 * chans * chans :].reshape(chans, chans)
    grad_padded = with_halo(grad_before, (("row", 1), ("col", 2)), DILATION)
    grad_pieces = jnp.stack(
        [
            window(grad_padded, 2 * DILATION - DILATION * a, 2 * DILATION - DILATION * b, rows, cols)
            for a in range(3)
            for b in range(3)
        ]
    )
    grad_active = jnp.einsum("tio,tohw->ihw", taps, grad_pieces, preferred_element_type=jnp.float32)
    grad_maps = (grad_wide + jnp.where(maps > 0, grad_active, 0.0)).astype(jnp.bfloat16)
    return (output, grad_maps, grad_kernel / map_bins, grad_mixing / map_bins)


def solution(mesh):
    placed = (P(None, "row", "col"), P(), P(), P(None, "row", "col"))
    return jax.shard_map(
        shards,
        mesh=mesh,
        in_specs=placed,
        out_specs=(P(None, "row", "col"), P(None, "row", "col"), P(), P()),
        check_vma=False,
    )
```

```python
import jax
import jax.numpy as jnp
from jax import lax
from jax.sharding import PartitionSpec as P

DILATION = 8


def with_halo(array, sides, width):
    for axis, dim in sides:
        peers, length = (lax.axis_size(axis), array.shape[dim])
        up = [(i, (i + 1) % peers) for i in range(peers - 1)]
        down = [(j, i) for i, j in up]
        last = lax.slice_in_dim(array, length - width, length, axis=dim)
        initial = lax.slice_in_dim(array, 0, width, axis=dim)
        if dim == array.ndim - 1:
            flat = last.shape[:-2] + (last.shape[-2] * width,)
            before = lax.ppermute(last.reshape(flat), axis, up).reshape(last.shape)
            after = lax.ppermute(initial.reshape(flat), axis, down).reshape(initial.shape)
        else:
            before = lax.ppermute(last, axis, up)
            after = lax.ppermute(initial, axis, down)
        array = jnp.concatenate([before, array, after], axis=dim)
    return array


RING_DIGITS = {"row": (2, 8, 2), "col": (4, 2)}


def gray(value):
    return value ^ (value >> 1)


def gray_inverse(value):
    result = 0
    while value:
        result ^= value
        value >>= 1
    return result


def ring_partner(index, digits, digit, bit):
    place = 1
    for size in digits[digit + 1 :]:
        place *= size
    value = index // place % digits[digit]
    flipped = gray(gray_inverse(value) ^ (1 << bit))
    return index + (flipped - value) * place


def all_sum(x, axes):
    for axis in axes:
        peers = lax.axis_size(axis)
        digits = RING_DIGITS.get(axis, (peers,))
        product = 1
        for size in digits:
            product *= size
        if product != peers or any(size & (size - 1) for size in digits):
            x = lax.psum(x, axis)
            continue
        for digit in reversed(range(len(digits))):
            for bit in range(digits[digit].bit_length() - 1):
                pairs = [(i, ring_partner(i, digits, digit, bit)) for i in range(peers)]
                x = x + lax.ppermute(x, axis, pairs)
    return x


def mirror_tile(tile):
    row_count = lax.axis_size("row")
    col_count = lax.axis_size("col")
    chans, rows, cols = tile.shape
    width = rows // col_count
    strip = lax.all_to_all(tile, "col", split_axis=1, concat_axis=2, tiled=True)
    blocks = lax.all_to_all(strip, "row", split_axis=2, concat_axis=1, tiled=True)
    turned = jnp.transpose(blocks.reshape(chans, row_count, width, rows), (0, 3, 1, 2))
    landed = lax.all_to_all(turned, "col", split_axis=2, concat_axis=3, tiled=True)
    return landed.reshape(chans, rows, cols)


def window(padded, top, left, rows, cols):
    return padded[:, top : top + rows, left : left + cols]


def shards(maps, kernel, mixing, cotangent):
    chans, rows, cols = maps.shape
    map_bins = rows * lax.axis_size("row")
    active = jnp.maximum(maps, 0)
    padded = with_halo(active, (("row", 1), ("col", 2)), DILATION)
    taps = kernel.reshape(9, chans, chans)
    pieces = jnp.stack(
        [window(padded, DILATION * a, DILATION * b, rows, cols) for a in range(3) for b in range(3)]
    )
    before = jnp.einsum("tio,tihw->ohw", taps, pieces, preferred_element_type=jnp.float32)
    hidden = jnp.maximum(before, 0.0).astype(jnp.bfloat16)
    mixed = jnp.einsum("io,ihw->ohw", mixing, hidden, preferred_element_type=jnp.float32).astype(
        jnp.bfloat16
    )
    mixed_turned = mirror_tile(mixed)
    grad_turned = mirror_tile(cotangent)
    output = (
        maps.astype(jnp.float32)
        + 0.5 * (mixed.astype(jnp.float32) + mixed_turned.astype(jnp.float32))
    ).astype(jnp.bfloat16)
    grad_wide = cotangent.astype(jnp.float32)
    grad_mixed = (0.5 * (grad_wide + grad_turned.astype(jnp.float32))).astype(jnp.bfloat16)
    local_mixing = jnp.einsum("ihw,ohw->io", hidden, grad_mixed, preferred_element_type=jnp.float32)
    grad_hidden = jnp.einsum("io,ohw->ihw", mixing, grad_mixed, preferred_element_type=jnp.float32)
    grad_before = jnp.where(hidden > 0, grad_hidden, 0.0).astype(jnp.bfloat16)
    local_kernel = jnp.einsum("tihw,ohw->tio", pieces, grad_before, preferred_element_type=jnp.float32)
    flat = jnp.concatenate([local_kernel.reshape(-1), local_mixing.reshape(-1)])
    sums = all_sum(flat.reshape(-1, 128), ("row", "col")).reshape(-1)
    grad_kernel = sums[: 9 * chans * chans].reshape(3, 3, chans, chans)
    grad_mixing = sums[9 * chans * chans :].reshape(chans, chans)
    grad_padded = with_halo(grad_before, (("row", 1), ("col", 2)), DILATION)
    grad_pieces = jnp.stack(
        [
            window(grad_padded, 2 * DILATION - DILATION * a, 2 * DILATION - DILATION * b, rows, cols)
            for a in range(3)
            for b in range(3)
        ]
    )
    grad_active = jnp.einsum("tio,tohw->ihw", taps, grad_pieces, preferred_element_type=jnp.float32)
    grad_maps = (grad_wide + jnp.where(maps > 0, grad_active, 0.0)).astype(jnp.bfloat16)
    return (output, grad_maps, grad_kernel / map_bins, grad_mixing / map_bins)


def solution(mesh):
    placed = (P(None, "row", "col"), P(), P(), P(None, "row", "col"))
    return jax.shard_map(
        shards,
        mesh=mesh,
        in_specs=placed,
        out_specs=(P(None, "row", "col"), P(None, "row", "col"), P(), P()),
        check_vma=False,
    )
```

```python
import jax
import jax.numpy as jnp
from jax import lax
from jax.sharding import PartitionSpec as P

DILATION = 8


def with_halo(array, sides, width):
    for axis, dim in sides:
        peers, length = (lax.axis_size(axis), array.shape[dim])
        up = [(i, (i + 1) % peers) for i in range(peers - 1)]
        down = [(j, i) for i, j in up]
        last = lax.slice_in_dim(array, length - width, length, axis=dim)
        initial = lax.slice_in_dim(array, 0, width, axis=dim)
        if dim == array.ndim - 1:
            flat = last.shape[:-2] + (last.shape[-2] * width,)
            before = lax.ppermute(last.reshape(flat), axis, up).reshape(last.shape)
            after = lax.ppermute(initial.reshape(flat), axis, down).reshape(initial.shape)
        else:
            before = lax.ppermute(last, axis, up)
            after = lax.ppermute(initial, axis, down)
        array = jnp.concatenate([before, array, after], axis=dim)
    return array


RING_DIGITS = {"row": (2, 8, 2), "col": (4, 2)}


def gray(value):
    return value ^ (value >> 1)


def gray_inverse(value):
    result = 0
    while value:
        result ^= value
        value >>= 1
    return result


def ring_partner(index, digits, digit, bit):
    place = 1
    for size in digits[digit + 1 :]:
        place *= size
    value = index // place % digits[digit]
    flipped = gray(gray_inverse(value) ^ (1 << bit))
    return index + (flipped - value) * place


def all_sum(x, axes):
    for axis in axes:
        peers = lax.axis_size(axis)
        digits = RING_DIGITS.get(axis, (peers,))
        product = 1
        for size in digits:
            product *= size
        if product != peers or any(size & (size - 1) for size in digits):
            x = lax.psum(x, axis)
            continue
        for digit in reversed(range(len(digits))):
            for bit in range(digits[digit].bit_length() - 1):
                pairs = [(i, ring_partner(i, digits, digit, bit)) for i in range(peers)]
                x = x + lax.ppermute(x, axis, pairs)
    return x


def mirror_tile(tile, strip=None):
    row_count = lax.axis_size("row")
    col_count = lax.axis_size("col")
    chans, rows, cols = tile.shape
    width = rows // col_count
    if strip is None:
        strip = lax.all_to_all(tile, "col", split_axis=1, concat_axis=2, tiled=True)
    blocks = lax.all_to_all(strip, "row", split_axis=2, concat_axis=1, tiled=True)
    turned = jnp.transpose(blocks.reshape(chans, row_count, width, rows), (0, 3, 1, 2))
    landed = lax.all_to_all(turned, "col", split_axis=2, concat_axis=3, tiled=True)
    return landed.reshape(chans, rows, cols)


def window(padded, top, left, rows, cols):
    return padded[:, top : top + rows, left : left + cols]


def shards(maps, kernel, mixing, cotangent):
    chans, rows, cols = maps.shape
    map_bins = rows * lax.axis_size("row")
    grad_strip = lax.all_to_all(cotangent, "col", split_axis=1, concat_axis=2, tiled=True)
    grad_strip, maps = lax.optimization_barrier((grad_strip, maps))
    active = jnp.maximum(maps, 0)
    padded = with_halo(active, (("row", 1), ("col", 2)), DILATION)
    taps = kernel.reshape(9, chans, chans)
    pieces = jnp.stack(
        [window(padded, DILATION * a, DILATION * b, rows, cols) for a in range(3) for b in range(3)]
    )
    before = jnp.einsum("tio,tihw->ohw", taps, pieces, preferred_element_type=jnp.float32)
    hidden = jnp.maximum(before, 0.0).astype(jnp.bfloat16)
    mixed = jnp.einsum("io,ihw->ohw", mixing, hidden, preferred_element_type=jnp.float32).astype(
        jnp.bfloat16
    )
    mixed_turned = mirror_tile(mixed)
    grad_turned = mirror_tile(cotangent, grad_strip)
    output = (
        maps.astype(jnp.float32)
        + 0.5 * (mixed.astype(jnp.float32) + mixed_turned.astype(jnp.float32))
    ).astype(jnp.bfloat16)
    grad_wide = cotangent.astype(jnp.float32)
    grad_mixed = (0.5 * (grad_wide + grad_turned.astype(jnp.float32))).astype(jnp.bfloat16)
    local_mixing = jnp.einsum("ihw,ohw->io", hidden, grad_mixed, preferred_element_type=jnp.float32)
    grad_hidden = jnp.einsum("io,ohw->ihw", mixing, grad_mixed, preferred_element_type=jnp.float32)
    grad_before = jnp.where(hidden > 0, grad_hidden, 0.0).astype(jnp.bfloat16)
    local_kernel = jnp.einsum("tihw,ohw->tio", pieces, grad_before, preferred_element_type=jnp.float32)
    flat = jnp.concatenate([local_kernel.reshape(-1), local_mixing.reshape(-1)])
    sums = all_sum(flat.reshape(-1, 128), ("row", "col")).reshape(-1)
    grad_kernel = sums[: 9 * chans * chans].reshape(3, 3, chans, chans)
    grad_mixing = sums[9 * chans * chans :].reshape(chans, chans)
    grad_padded = with_halo(grad_before, (("row", 1), ("col", 2)), DILATION)
    grad_pieces = jnp.stack(
        [
            window(grad_padded, 2 * DILATION - DILATION * a, 2 * DILATION - DILATION * b, rows, cols)
            for a in range(3)
            for b in range(3)
        ]
    )
    grad_active = jnp.einsum("tio,tohw->ihw", taps, grad_pieces, preferred_element_type=jnp.float32)
    grad_maps = (grad_wide + jnp.where(maps > 0, grad_active, 0.0)).astype(jnp.bfloat16)
    return (output, grad_maps, grad_kernel / map_bins, grad_mixing / map_bins)


def solution(mesh):
    placed = (P(None, "row", "col"), P(), P(), P(None, "row", "col"))
    return jax.shard_map(
        shards,
        mesh=mesh,
        in_specs=placed,
        out_specs=(P(None, "row", "col"), P(None, "row", "col"), P(), P()),
        check_vma=False,
    )
```

```python
import jax
import jax.numpy as jnp
from jax import lax
from jax.sharding import PartitionSpec as P

DILATION = 8


def with_halo(array, sides, width):
    for axis, dim in sides:
        peers, length = (lax.axis_size(axis), array.shape[dim])
        up = [(i, (i + 1) % peers) for i in range(peers - 1)]
        down = [(j, i) for i, j in up]
        last = lax.slice_in_dim(array, length - width, length, axis=dim)
        initial = lax.slice_in_dim(array, 0, width, axis=dim)
        if dim == array.ndim - 1:
            flat = last.shape[:-2] + (last.shape[-2] * width,)
            before = lax.ppermute(last.reshape(flat), axis, up).reshape(last.shape)
            after = lax.ppermute(initial.reshape(flat), axis, down).reshape(initial.shape)
        else:
            before = lax.ppermute(last, axis, up)
            after = lax.ppermute(initial, axis, down)
        array = jnp.concatenate([before, array, after], axis=dim)
    return array


RING_DIGITS = {"row": (2, 8, 2), "col": (4, 2)}


def gray(value):
    return value ^ (value >> 1)


def gray_inverse(value):
    result = 0
    while value:
        result ^= value
        value >>= 1
    return result


def ring_partner(index, digits, digit, bit):
    place = 1
    for size in digits[digit + 1 :]:
        place *= size
    value = index // place % digits[digit]
    flipped = gray(gray_inverse(value) ^ (1 << bit))
    return index + (flipped - value) * place


def all_sum(x, axes):
    for axis in axes:
        peers = lax.axis_size(axis)
        digits = RING_DIGITS.get(axis, (peers,))
        product = 1
        for size in digits:
            product *= size
        if product != peers or any(size & (size - 1) for size in digits):
            x = lax.psum(x, axis)
            continue
        for digit in reversed(range(len(digits))):
            for bit in range(digits[digit].bit_length() - 1):
                pairs = [(i, ring_partner(i, digits, digit, bit)) for i in range(peers)]
                x = x + lax.ppermute(x, axis, pairs)
    return x


def mirror_tile(tile):
    row_count = lax.axis_size("row")
    col_count = lax.axis_size("col")
    chans, rows, cols = tile.shape
    width = rows // col_count
    strip = lax.all_to_all(tile, "col", split_axis=1, concat_axis=2, tiled=True)
    blocks = lax.all_to_all(strip, "row", split_axis=2, concat_axis=1, tiled=True)
    turned = jnp.transpose(blocks.reshape(chans, row_count, width, rows), (0, 3, 1, 2))
    landed = lax.all_to_all(turned, "col", split_axis=2, concat_axis=3, tiled=True)
    return landed.reshape(chans, rows, cols)


def window(padded, top, left, rows, cols):
    return padded[:, top : top + rows, left : left + cols]


def shards(maps, kernel, mixing, cotangent):
    chans, rows, cols = maps.shape
    map_bins = rows * lax.axis_size("row")
    active = jnp.maximum(maps, 0)
    padded = with_halo(active, (("row", 1), ("col", 2)), DILATION)
    taps = kernel.reshape(9, chans, chans)
    pieces = jnp.stack(
        [window(padded, DILATION * a, DILATION * b, rows, cols) for a in range(3) for b in range(3)]
    )
    before = jnp.einsum("tio,tihw->ohw", taps, pieces, preferred_element_type=jnp.float32)
    hidden = jnp.maximum(before, 0.0).astype(jnp.bfloat16)
    mixed = jnp.einsum("io,ihw->ohw", mixing, hidden, preferred_element_type=jnp.float32).astype(
        jnp.bfloat16
    )
    mixed_turned = mirror_tile(mixed)
    grad_turned = mirror_tile(cotangent)
    output = (
        maps.astype(jnp.float32)
        + 0.5 * (mixed.astype(jnp.float32) + mixed_turned.astype(jnp.float32))
    ).astype(jnp.bfloat16)
    grad_wide = cotangent.astype(jnp.float32)
    grad_mixed = (0.5 * (grad_wide + grad_turned.astype(jnp.float32))).astype(jnp.bfloat16)
    local_mixing = jnp.einsum("ihw,ohw->io", hidden, grad_mixed, preferred_element_type=jnp.float32)
    grad_hidden = jnp.einsum("io,ohw->ihw", mixing, grad_mixed, preferred_element_type=jnp.float32)
    grad_before = jnp.where(hidden > 0, grad_hidden, 0.0).astype(jnp.bfloat16)
    local_kernel = jnp.einsum("tihw,ohw->tio", pieces, grad_before, preferred_element_type=jnp.float32)
    flat = jnp.concatenate([local_kernel.reshape(-1), local_mixing.reshape(-1)]) / map_bins
    sums = all_sum(flat.reshape(-1, 128), ("row", "col")).reshape(-1)
    grad_kernel = sums[: 9 * chans * chans].reshape(3, 3, chans, chans)
    grad_mixing = sums[9 * chans * chans :].reshape(chans, chans)
    grad_padded = with_halo(grad_before, (("row", 1), ("col", 2)), DILATION)
    grad_pieces = jnp.stack(
        [
            window(grad_padded, 2 * DILATION - DILATION * a, 2 * DILATION - DILATION * b, rows, cols)
            for a in range(3)
            for b in range(3)
        ]
    )
    grad_active = jnp.einsum("tio,tohw->ihw", taps, grad_pieces, preferred_element_type=jnp.float32)
    grad_maps = (grad_wide + jnp.where(maps > 0, grad_active, 0.0)).astype(jnp.bfloat16)
    return (output, grad_maps, grad_kernel, grad_mixing)


def solution(mesh):
    placed = (P(None, "row", "col"), P(), P(), P(None, "row", "col"))
    return jax.shard_map(
        shards,
        mesh=mesh,
        in_specs=placed,
        out_specs=(P(None, "row", "col"), P(None, "row", "col"), P(), P()),
        check_vma=False,
    )
```
